32 devices in a mesh: groups: 2 (over x), tok: 16 (over z, y, core).
Axes of the slice: x: 2, y: 2, z: 4, core: 2. Of those that a mesh axis runs over, the one named last changes fastest.
Arguments:
- tokens: bfloat16 [4096, 3072], P(('groups', 'tok')), parts along dimension 0, may hold values from -6 to 6
- routes: int32 [4096, 2], P(('groups', 'tok')), parts along dimension 0, may hold values from 0 to 7, all different within a row; in each aligned block of 128 rows (0 to 127, 128 to 255, ...) at most 40 rows name the same one
- weights: bfloat16 [32768, 3072], P(('groups', 'tok')), parts along dimension 0, may hold values from -0.109375 to 0.109375
Outputs:
- whitened: bfloat16 [32768, 3072], P(('groups', 'tok')), parts along dimension 0
The draws below stay inside these ranges and needn't reach their ends.
There are 2 independent parts, one for each index of `groups`. The reference program is written for one: setup_inputs(seed, part) draws one part's arguments, and reference() takes and returns one part's arrays. A program takes and returns all parts, laid end to end along the dimension named above; each array names one. Nothing has to cross between parts.
Inputs may be any that keep to these rules, and one draw needn't show every extreme that they name: `routes`: each token names 2 different experts. Within the tokens of one device no expert is named more than 40 times, and in every draw some expert is named exactly 40 times by the tokens of some device.
All inputs are finite; a program needn't handle non-finite values.
Results may differ from the reference program's by a relative error of at most 0.0064.
The reference program's roundings to bfloat16 on the way (of `expert_rows` and `lower`) count: a program that leaves them out, or rounds other values in their place, can miss the bound.
Values may be sent and summed in bfloat16 or wider, within the bound.
A program may use at most 256 MiB of HBM per device.

```python
import math
import jax
import jax.numpy as jnp
import numpy as np
from jax import lax

D = 3072
E = 8
TOP = 2
FF_DEV = 1024
NB = 4
TOK_DEV = 128
MOST = 40
FF = 2048
TOKENS = 2048
N_TOK = 16


def level_of(key, shape, shards, smallest, largest):
    loudness, own = 1.0, jax.random.fold_in(key, 6)
    for axis_at, parts in shards:
        draws = jnp.exp(jax.random.uniform(jax.random.fold_in(own, axis_at), (parts,), jnp.float32, smallest / len(shards), largest / len(shards)))
        loudness = loudness * jnp.repeat(draws, shape[axis_at] // parts).reshape([-1 if axis == axis_at else 1 for axis in range(len(shape))])
    return loudness


def assign_block(own_key, own, number, rows, count, top, reach, skew):
    ranking = jax.random.permutation(own_key, count)
    packed, common = shares(count, rows * top, reach, skew, True), shares(count, rows * top, reach, skew, False)
    places = jnp.arange(count)

    def named(sizes, offset_by):
        used = int((sizes > 0).sum())
        fixed = max(1, used // 4)
        shifted = fixed + (places - fixed + offset_by * (used - fixed)) % max(1, count - fixed)
        return jnp.zeros((count,), jnp.int32).at[ranking[jnp.where(places < fixed, places, shifted)]].set(jnp.asarray(sizes, jnp.int32))

    sizes = jnp.where(number % 4 == 0, named(packed, number // 4), named(common, number - number // 4 - 1))
    mixed = jax.random.permutation(jax.random.fold_in(own, 3), count)
    donor, taker = mixed[0:count // 2 * 2:2], mixed[1:count // 2 * 2:2]
    margin = jnp.minimum(sizes[donor] - 1, reach - sizes[taker]) // 2
    margin = jnp.where((donor == ranking[0]) | (taker == ranking[0]) | (sizes[taker] == 0), 0, jnp.maximum(margin, 0))
    shifted = jax.random.randint(jax.random.fold_in(own, 4), (count // 2,), 0, 1 << 20) % (margin + 1)
    sizes = sizes.at[donor].add(-shifted).at[taker].add(shifted)
    members = jnp.searchsorted(jnp.cumsum(sizes), jnp.arange(rows * top), side="right").astype(jnp.int32)
    grid = members.reshape(top, rows).T
    grid = grid[jax.random.permutation(jax.random.fold_in(own, 1), rows)]
    offset_by = jax.random.randint(jax.random.fold_in(own, 2), (rows, 1), 0, top)
    return jnp.take_along_axis(grid, (jnp.arange(top)[None, :] + offset_by) % top, axis=1)


def shares(number_of, total, most, lean, full):
    portions = [(1 << 20) // math.isqrt(standing ** lean) + 1 for standing in range(1, number_of + 1)]
    largest = most if full else min(most, max(-(-total // number_of), total * portions[0] // sum(portions)))
    least = 1 if total - largest >= number_of - 1 else 0
    given, spare = [largest] + [least] * (number_of - 1), total - largest - least * (number_of - 1)
    while spare > 0:
        free = [i for i in range(1, number_of) if given[i] < largest] or [i for i in range(1, number_of) if given[i] < most]
        mass, remaining = sum([portions[i] for i in free]), spare
        for i in free:
            addition = min(most - given[i], max(1, remaining * portions[i] // mass), spare)
            given[i] = given[i] + addition
            spare = spare - addition
    return np.array(given)


def scatter_about(rng, shape, deviation, bound, shards=(), kind=jnp.bfloat16):
    level = level_of(rng, shape, shards, -0.22, 0.18) if shards else 1.0
    entries = jax.random.normal(rng, shape, jnp.float32) * deviation * level
    return jnp.minimum(jnp.maximum(entries, -bound), bound).astype(kind)


def setup_inputs(seed: int = 0, part: int = 0) -> dict:
    key_list = jax.random.split(jax.random.key(seed), 4)
    part_splits = jax.random.split(jax.random.fold_in(key_list[3], part), 4)
    tokens = scatter_about(part_splits[0], (TOKENS, D), 1.0, 6.0, ((0, 16),))
    routes_keys = jax.random.split(jax.random.fold_in(part_splits[1], 1), TOKENS // TOK_DEV)
    routes_turns = jax.random.permutation(jax.random.fold_in(part_splits[1], 3), TOKENS // TOK_DEV)
    routes = jax.vmap(lambda own, number: assign_block(jax.random.fold_in(part_splits[1], 2), own, number, TOK_DEV, E, TOP, MOST, 2))(routes_keys, routes_turns).reshape((TOKENS, TOP))
    weights = scatter_about(part_splits[2], (E * FF, D), D ** -0.5, 0.109375, ((0, 16),))
    return {"tokens": tokens, "routes": routes, "weights": weights}


damping = 256.0

def reference(tokens, routes, weights):
    slices = N_TOK // E
    hidden = FF_DEV * slices
    cap_rows = N_TOK * MOST
    band_width = D // NB
    results = []
    for expert in range(E):
        hit_count = jnp.sum((routes == expert).astype(jnp.int32), axis=1)
        row_index = jnp.nonzero(hit_count > 0, size=cap_rows, fill_value=0)[0].astype(jnp.int32)
        valid_rows = jnp.arange(cap_rows, dtype=jnp.int32) < jnp.sum(hit_count)
        expert_rows = jnp.where(valid_rows[:, None], tokens[row_index], jnp.zeros((), tokens.dtype))
        gram_matrix = lax.dot_general(expert_rows.astype(jnp.float32), expert_rows.astype(jnp.float32), (((0,), (0,)), ((), ())), preferred_element_type=jnp.float32)
        lower_bf = jnp.zeros((D, D), jnp.bfloat16)
        for section in range(NB):
            lo_col = section * band_width
            hi_col = lo_col + band_width
            column_block = gram_matrix[lo_col:, lo_col:hi_col]
            if section > 0:
                column_block = column_block - lax.dot_general(lower_bf[lo_col:, :lo_col].astype(jnp.float32), lower_bf[lo_col:hi_col, :lo_col].astype(jnp.float32), (((1,), (1,)), ((), ())), preferred_element_type=jnp.float32)
            diag_block = column_block[:band_width] + damping * jnp.eye(band_width, dtype=jnp.float32)
            diag_factor = jnp.linalg.cholesky(diag_block)
            stacked = diag_factor
            if section + 1 < NB:
                below_rows = lax.linalg.triangular_solve(diag_factor, column_block[band_width:], left_side=False, lower=True, transpose_a=True)
                stacked = jnp.concatenate([diag_factor, below_rows], 0)
            lower_bf = lower_bf.at[lo_col:, lo_col:hi_col].set(stacked.astype(jnp.bfloat16))
        expert_weight = weights[expert * hidden:(expert + 1) * hidden]
        results.append(jnp.dot(expert_weight.astype(jnp.float32), lower_bf.astype(jnp.float32), preferred_element_type=jnp.float32).astype(jnp.bfloat16))
    return jnp.concatenate(results, 0)
```

```python
import functools

import jax
import jax.numpy as jnp
from jax import lax
from jax.experimental import pallas as pl
from jax.experimental.pallas import tpu as pltpu
from jax.sharding import PartitionSpec as P

E = 8
NB = 4
BLK = 128
TILE = 256
HALF = 64

damping = 256.0


def exchange_kernel(slices, groups, per, packed, out, own_sem, send, recv, pass_send, pass_recv):
    count, most, _ = out.shape
    me = lax.axis_index("tok")
    mine = lax.rem(me, slices)
    expert = me // slices
    sizes = [max(0, min(per, most - s * per)) for s in range(slices)]
    barrier = pltpu.get_barrier_semaphore()
    for d in range(1, count):
        pl.semaphore_signal(
            barrier,
            inc=1,
            device_id={"tok": lax.rem(me + d, count)},
            device_id_type=pl.DeviceIdType.MESH,
        )
    pl.semaphore_wait(barrier, count - 1)

    def routed(eo, s, size, recv_slot):
        to = lax.rem(expert + eo, E)
        return pltpu.make_async_remote_copy(
            src_ref=packed.at[to, pl.ds(s * per, size)],
            dst_ref=out.at[eo * slices + mine, pl.ds(s * per, size)],
            send_sem=send.at[eo, s],
            recv_sem=recv.at[eo, recv_slot],
            device_id={"tok": to * slices + s},
            device_id_type=pl.DeviceIdType.MESH,
        )

    def shared(p, s, q, size, sem_slot):
        part = (pl.ds(q * count // groups, count // groups), pl.ds(s * per, size))
        return pltpu.make_async_remote_copy(
            src_ref=out.at[part],
            dst_ref=out.at[part],
            send_sem=pass_send.at[p, q],
            recv_sem=pass_recv.at[sem_slot, q],
            device_id={"tok": expert * slices + p},
            device_id_type=pl.DeviceIdType.MESH,
        )

    for eo in [*range(1, E), 0]:
        for s, size in enumerate(sizes):
            if size and eo:
                routed(eo, s, size, mine).start()
            elif size:

                @pl.when(mine != s)
                def _(s=s, size=size):
                    routed(0, s, size, mine).start()

                @pl.when(mine == s)
                def _(s=s, size=size):
                    own = pltpu.make_async_copy(
                        packed.at[expert, pl.ds(s * per, size)],
                        out.at[mine, pl.ds(s * per, size)],
                        own_sem,
                    )
                    own.start()
                    own.wait()

    for s, size in enumerate(sizes):
        if size:

            @pl.when(mine == s)
            def _(s=s, size=size):
                for q in range(groups):
                    for eo in range(q * E // groups, (q + 1) * E // groups):
                        for other in range(slices):
                            if eo or other != s:
                                routed(eo, s, size, other).wait_recv()
                    for p in range(slices):
                        if p != s:
                            shared(p, s, q, size, s).start()

    for eo in range(E):
        for s, size in enumerate(sizes):
            if size and eo:
                routed(eo, s, size, mine).wait_send()
            elif size:

                @pl.when(mine != s)
                def _(s=s, size=size):
                    routed(0, s, size, mine).wait_send()

    for s, size in enumerate(sizes):
        if size:

            @pl.when(mine == s)
            def _(s=s, size=size):
                for q in range(groups):
                    for p in range(slices):
                        if p != s:
                            shared(p, s, q, size, s).wait_send()

            @pl.when(mine != s)
            def _(s=s, size=size):
                for q in range(groups):
                    shared(s, s, q, size, s).wait_recv()


def exchange(packed, count):
    _, most, features = packed.shape
    slices = count // E
    groups = 4
    per = -(-most // 8 // slices) * 8
    return pl.pallas_call(
        functools.partial(exchange_kernel, slices, groups, per),
        out_shape=jax.ShapeDtypeStruct((count, most, features), packed.dtype),
        in_specs=[pl.BlockSpec(memory_space=pltpu.HBM)],
        out_specs=pl.BlockSpec(memory_space=pltpu.HBM),
        scratch_shapes=[
            pltpu.SemaphoreType.DMA,
            pltpu.SemaphoreType.DMA((E, slices)),
            pltpu.SemaphoreType.DMA((E, slices)),
            pltpu.SemaphoreType.DMA((slices, groups)),
            pltpu.SemaphoreType.DMA((slices, groups)),
        ],
        compiler_params=pltpu.CompilerParams(collective_id=0, has_side_effects=True),
    )(packed)


def slot_rows(target, slot_total, tokens):
    tok_rows = tokens.shape[0]
    slot_table = (target[None, :] == jnp.arange(slot_total, dtype=jnp.int32)[:, None]).astype(
        jnp.int32
    )
    slot_table = jnp.sum(slot_table.reshape(slot_total, tok_rows, 2), axis=2).astype(jnp.bfloat16)
    return jnp.dot(slot_table, tokens, preferred_element_type=jnp.float32).astype(jnp.bfloat16)


def spread(row):
    return jnp.broadcast_to(row, (8, BLK))


def split(value):
    high = value.astype(jnp.bfloat16)
    return high, (value - high.astype(jnp.float32)).astype(jnp.bfloat16)


def tn(a, b):
    return lax.dot_general(a, b, (((0,), (0,)), ((), ())), preferred_element_type=jnp.float32)


def inverse_factor(block_ref, inv_ref, beside):
    lane = lax.broadcasted_iota(jnp.int32, (8, BLK), 1)
    sub = lax.broadcasted_iota(jnp.int32, (8, BLK), 0)
    rest = [block_ref[8 * r : 8 * r + 8, :] for r in range(BLK // 8)]
    count = HALF // 8
    for s in range(BLK // HALF):
        rows, rest = rest[:count], rest[count:]
        dones = []
        for g in range(count):
            first = s * HALF + 8 * g
            inside = (lane >= first) & (lane < first + 8)
            cols = {
                r: [spread_lane(rows[r], first + j) for j in range(8)] for r in range(g, count)
            }
            own = jnp.where(inside, jnp.where(lane == first + sub, 1.0, 0.0), rows[g])
            diag = list(cols[g])
            done = jnp.zeros((8, BLK), jnp.float32)
            for j in range(0, 8, 2):
                u, v = diag[j], diag[j + 1]
                a, b, c = spread(u[j : j + 1]), spread(u[j + 1 : j + 2]), spread(v[j + 1 : j + 2])
                det = a * c - b * b
                recip = 1.0 / det
                root_a = lax.rsqrt(a)
                root_det = lax.rsqrt(det)
                at0, at1 = sub == j, sub == j + 1
                x, y = spread(own[j : j + 1]), spread(own[j + 1 : j + 2])
                lower = a * y - b * x
                upper = c * x - b * y
                done = jnp.where(at0, x * root_a, jnp.where(at1, lower * (root_a * root_det), done))
                sx, sy = upper * recip, lower * recip
                own = jnp.where(at0, sx, jnp.where(at1, sy, own - (u * sx + v * sy)))
                for m in range(j + 2, 8):
                    um, vm = spread(diag[m][j : j + 1]), spread(diag[m][j + 1 : j + 2])
                    p, q = c * um - b * vm, a * vm - b * um
                    w = jnp.where(at0, -p, jnp.where(at1, -q, u * p + v * q))
                    diag[m] = jnp.where(at0 | at1, 0.0, diag[m]) - w * recip
            inv_ref[first : first + 8, :] = jnp.where(lane <= first + sub, done, 0.0)
            dones.append(done)
            parts = [spread(own[j : j + 1, :]) for j in range(8)]
            for r in range(g + 1, count):
                t = [cols[r][j] * parts[j] for j in range(8)]
                t = ((t[0] + t[1]) + (t[2] + t[3])) + ((t[4] + t[5]) + (t[6] + t[7]))
                rows[r] = jnp.where(inside, 0.0, rows[r]) - t
            beside(s * count + g)
        if rest:
            low, top = s * HALF, (s + 1) * HALF
            col = lax.broadcasted_iota(jnp.int32, (HALF, BLK), 1)
            row = lax.broadcasted_iota(jnp.int32, (HALF, BLK), 0) + low
            high, less = split(jnp.where((col <= row) | (col >= top), jnp.concatenate(dones, 0), 0.0))
            taken = tn(jnp.concatenate([high, less, high], 0), jnp.concatenate([high, high, less], 0))
            within = (lane >= low) & (lane < top)
            rest = [
                jnp.where(within, 0.0, value) - taken[top + 8 * r : top + 8 * r + 8, :]
                for r, value in enumerate(rest)
            ]


def spread_lane(value, at):
    return jnp.broadcast_to(value[:, at : at + 1], (8, BLK))


def solve(left, tile):
    high, low = split(tile)
    return jnp.dot(
        left, jnp.concatenate([high, low, high], 0), preferred_element_type=jnp.float32
    )


def upper_part(value, first_row, first_col):
    row = first_row + lax.broadcasted_iota(jnp.int32, value.shape, 0)
    col = first_col + lax.broadcasted_iota(jnp.int32, value.shape, 1)
    return jnp.where(col >= row, value, 0.0).astype(jnp.bfloat16)


def damped(value, first_row, first_col):
    row = first_row + lax.broadcasted_iota(jnp.int32, value.shape, 0)
    col = first_col + lax.broadcasted_iota(jnp.int32, value.shape, 1)
    return value + jnp.where(row == col, damping, 0.0)


def factor_kernel(x_ref, u_ref, wide, panel, early, lefts, inv_ref, block_ref):
    features = x_ref.shape[1]
    width = features // NB
    panels = width // BLK
    tiles = [slice(t, t + TILE) for t in range(0, width, TILE)]
    half = panels // 2
    panel[...] = jnp.zeros_like(panel)
    lefts[features // BLK] = jnp.zeros(lefts.shape[1:], jnp.bfloat16)

    def clear(r, c):
        u_ref[pl.ds(pl.multiple_of(r * BLK, BLK), BLK), :] = jnp.zeros((BLK, features), jnp.bfloat16)
        return c

    lax.fori_loop(0, features // BLK + 1, clear, 0)

    def at(start, size=BLK):
        return pl.ds(pl.multiple_of(start, BLK), size)

    def ahead(q, cols, deep):
        rows = at(q * BLK)
        value = tn(x_ref[:, rows], x_ref[:, cols])
        if deep:
            value = value - tn(u_ref[:deep, rows], u_ref[:deep, cols])
        u_ref[rows, cols] = solve(lefts[q], value).astype(jnp.bfloat16)

    def gram(slot, cols, own, deep):
        value = tn(x_ref[:, own], x_ref[:, cols])
        if deep:
            value = value - tn(u_ref[:deep, own], u_ref[:deep, cols])
        wide[slot, :, pl.ds(cols.start - own.start, cols.size)] = value

    for t in tiles:
        gram(0, pl.ds(t.start, TILE), pl.ds(0, width), 0)

    def first_block(k):
        low = k * width
        block_ref[...] = damped(wide[k % 2, 0:BLK, 0:BLK], 0, 0)

    def in_band(k, i, extra):
        low = k * width
        band = slice(low, low + width)
        start = low + i * BLK
        p = k * panels + i
        nxt = jnp.minimum(i + 1, panels - 1)
        nxt_at = at(low + nxt * BLK)
        last_row = jnp.where(i == 0, features, start - BLK)
        last_left = jnp.where(i == 0, features // BLK, p - 1)
        tasks = []

        def settle(t):
            value = solve(lefts[last_left], panel[:, t])
            u_ref[at(last_row), low + t.start : low + t.stop] = upper_part(
                value, start - BLK, low + t.start
            )

        def renew(t):
            cols = slice(low + t.start, low + t.stop)
            value = wide[k % 2, at(i * BLK), t] - tn(u_ref[band, at(start)], u_ref[band, cols])
            panel[:, t] = damped(value, start, low + t.start)

        def look():
            early[...] = damped(wide[k % 2, at(nxt * BLK), at(nxt * BLK)], 0, 0) - tn(
                u_ref[band, nxt_at], u_ref[band, nxt_at]
            )

        for t in tiles:
            tasks.append(functools.partial(settle, t))
        for t in tiles:
            tasks.append(functools.partial(renew, t))
        tasks.append(look)
        tasks += extra
        slots = BLK // 8

        def beside(g):
            for n, task in enumerate(tasks):
                if n * slots // len(tasks) == g:
                    task()

        inverse_factor(block_ref, inv_ref, beside)
        high, rest = split(inv_ref[...])
        left = jnp.concatenate([high, high, rest], 1)
        lefts[p] = left
        near = upper_part(solve(left, panel[:, at(nxt * BLK)]), start, low + nxt * BLK)
        u_ref[at(start), nxt_at] = near
        block_ref[...] = early[...] - tn(near, near)

    for k in range(NB):
        low, high = k * width, (k + 1) * width
        first_block(k)
        old = k * panels
        cols = [pl.ds(high + t.start, TILE) for t in tiles]
        more = k + 1 < NB

        def old_step(i, c):
            extra = []
            if more:
                each = old // half
                for r in range(each):
                    for col in cols:
                        extra.append(functools.partial(ahead, i * each + r, col, low))
            in_band(k, i, extra)
            return c

        def new_step(i, c):
            extra = []
            if more:
                j = i - half
                for r in range(2):
                    for col in cols:
                        extra.append(functools.partial(ahead, old + 2 * j + r, col, high))
            in_band(k, i, extra)
            return c

        def single_step(i, c):
            in_band(k, i, [])
            return c

        if more:
            lax.fori_loop(0, half, old_step, 0)
            lax.fori_loop(half, panels - 1, new_step, 0)
            in_band(
                k,
                panels - 1,
                [functools.partial(ahead, old + panels - 2, col, high) for col in cols]
                + [
                    functools.partial(gram, (k + 1) % 2, col, pl.ds(high, width), low)
                    for col in cols
                ],
            )
            for col in cols:
                ahead(old + panels - 1, col, high)
            for col in cols:
                wide[(k + 1) % 2, :, pl.ds(col.start - high, TILE)] -= tn(
                    u_ref[low:high, pl.ds(high, width)], u_ref[low:high, col]
                )
        else:
            lax.fori_loop(0, panels, single_step, 0)


def upper_factor(gathered):
    rows, features = gathered.shape
    width = features // NB
    return pl.pallas_call(
        factor_kernel,
        out_shape=jax.ShapeDtypeStruct((features + BLK, features), jnp.bfloat16),
        in_specs=[pl.BlockSpec(memory_space=pltpu.VMEM)],
        out_specs=pl.BlockSpec(memory_space=pltpu.VMEM),
        scratch_shapes=[
            pltpu.VMEM((2, width, width), jnp.float32),
            pltpu.VMEM((BLK, width), jnp.float32),
            pltpu.VMEM((BLK, BLK), jnp.float32),
            pltpu.VMEM((features // BLK + 1, BLK, 3 * BLK), jnp.bfloat16),
            pltpu.VMEM((BLK, BLK), jnp.float32),
            pltpu.VMEM((BLK, BLK), jnp.float32),
        ],
        compiler_params=pltpu.CompilerParams(vmem_limit_bytes=63 << 20),
    )(gathered)


def whiten_kernel(columns, w_ref, u_ref, out_ref):
    features = w_ref.shape[1]
    for t in range(features // columns):

        @pl.when(pl.program_id(1) == t)
        def _():
            out_ref[...] = lax.dot_general(
                w_ref[:, t * columns :],
                u_ref[:, t * columns :],
                (((1,), (1,)), ((), ())),
                preferred_element_type=jnp.float32,
            ).astype(jnp.bfloat16)


def whiten(weights, upper):
    hidden, features = weights.shape
    columns, block = 512, min(1024, hidden)
    return pl.pallas_call(
        functools.partial(whiten_kernel, columns),
        out_shape=jax.ShapeDtypeStruct((hidden, features), jnp.bfloat16),
        grid=(hidden // block, features // columns),
        in_specs=[
            pl.BlockSpec((block, features), lambda i, t: (i, 0)),
            pl.BlockSpec((columns, features), lambda i, t: (t, 0)),
        ],
        out_specs=pl.BlockSpec((block, columns), lambda i, t: (i, t)),
        compiler_params=pltpu.CompilerParams(vmem_limit_bytes=48 << 20),
    )(weights, upper)


def local(tokens, routes, weights):
    tok_devices = lax.axis_size("tok")
    tok_rows = tokens.shape[0]
    features = tokens.shape[1]
    most_rows = tok_rows * 5 // 16
    picked = routes.reshape(-1)
    onehot = (picked[:, None] == jnp.arange(E, dtype=jnp.int32)[None, :]).astype(jnp.bfloat16)
    place = jnp.arange(2 * tok_rows, dtype=jnp.int32)
    earlier = (place[:, None] > place[None, :]).astype(jnp.bfloat16)
    before = jnp.dot(earlier, onehot, preferred_element_type=jnp.float32)
    ranked = jnp.sum(before * onehot.astype(jnp.float32), axis=1).astype(jnp.int32)
    packed = slot_rows(picked * most_rows + ranked, E * most_rows, tokens)
    gathered = exchange(packed.reshape(E, most_rows, features), tok_devices)
    upper = upper_factor(gathered.reshape(tok_devices * most_rows, features))
    return whiten(weights, upper)


def solution(mesh):
    return jax.shard_map(
        local,
        mesh=mesh,
        in_specs=(
            P(("groups", "tok"), None),
            P(("groups", "tok"), None),
            P(("groups", "tok"), None),
        ),
        out_specs=P(("groups", "tok"), None),
        check_vma=False,
    )
```

```python
import functools

import jax
import jax.numpy as jnp
from jax import lax
from jax.experimental import pallas as pl
from jax.experimental.pallas import tpu as pltpu
from jax.sharding import PartitionSpec as P

E = 8
NB = 4
BLK = 128
TILE = 256
HALF = 64

damping = 256.0


def exchange_kernel(slices, groups, per, packed, out, own_sem, send, recv, pass_send, pass_recv):
    count, most, _ = out.shape
    me = lax.axis_index("tok")
    mine = lax.rem(me, slices)
    expert = me // slices
    sizes = [max(0, min(per, most - s * per)) for s in range(slices)]
    barrier = pltpu.get_barrier_semaphore()
    for d in range(1, count):
        pl.semaphore_signal(
            barrier,
            inc=1,
            device_id={"tok": lax.rem(me + d, count)},
            device_id_type=pl.DeviceIdType.MESH,
        )
    pl.semaphore_wait(barrier, count - 1)

    def routed(eo, s, size, recv_slot):
        to = lax.rem(expert + eo, E)
        return pltpu.make_async_remote_copy(
            src_ref=packed.at[to, pl.ds(s * per, size)],
            dst_ref=out.at[eo * slices + mine, pl.ds(s * per, size)],
            send_sem=send.at[eo, s],
            recv_sem=recv.at[eo, recv_slot],
            device_id={"tok": to * slices + s},
            device_id_type=pl.DeviceIdType.MESH,
        )

    def shared(p, s, q, size, sem_slot):
        part = (pl.ds(q * count // groups, count // groups), pl.ds(s * per, size))
        return pltpu.make_async_remote_copy(
            src_ref=out.at[part],
            dst_ref=out.at[part],
            send_sem=pass_send.at[p, q],
            recv_sem=pass_recv.at[sem_slot, q],
            device_id={"tok": expert * slices + p},
            device_id_type=pl.DeviceIdType.MESH,
        )

    for eo in [*range(1, E), 0]:
        for s, size in enumerate(sizes):
            if size and eo:
                routed(eo, s, size, mine).start()
            elif size:

                @pl.when(mine != s)
                def _(s=s, size=size):
                    routed(0, s, size, mine).start()

                @pl.when(mine == s)
                def _(s=s, size=size):
                    own = pltpu.make_async_copy(
                        packed.at[expert, pl.ds(s * per, size)],
                        out.at[mine, pl.ds(s * per, size)],
                        own_sem,
                    )
                    own.start()
                    own.wait()

    for s, size in enumerate(sizes):
        if size:

            @pl.when(mine == s)
            def _(s=s, size=size):
                for q in range(groups):
                    for eo in range(q * E // groups, (q + 1) * E // groups):
                        for other in range(slices):
                            if eo or other != s:
                                routed(eo, s, size, other).wait_recv()
                    for p in range(slices):
                        if p != s:
                            shared(p, s, q, size, s).start()

    for eo in range(E):
        for s, size in enumerate(sizes):
            if size and eo:
                routed(eo, s, size, mine).wait_send()
            elif size:

                @pl.when(mine != s)
                def _(s=s, size=size):
                    routed(0, s, size, mine).wait_send()

    for s, size in enumerate(sizes):
        if size:

            @pl.when(mine == s)
            def _(s=s, size=size):
                for q in range(groups):
                    for p in range(slices):
                        if p != s:
                            shared(p, s, q, size, s).wait_send()

            @pl.when(mine != s)
            def _(s=s, size=size):
                for q in range(groups):
                    shared(s, s, q, size, s).wait_recv()


def exchange(packed, count):
    _, most, features = packed.shape
    slices = count // E
    groups = 4
    per = -(-most // 8 // slices) * 8
    return pl.pallas_call(
        functools.partial(exchange_kernel, slices, groups, per),
        out_shape=jax.ShapeDtypeStruct((count, most, features), packed.dtype),
        in_specs=[pl.BlockSpec(memory_space=pltpu.HBM)],
        out_specs=pl.BlockSpec(memory_space=pltpu.HBM),
        scratch_shapes=[
            pltpu.SemaphoreType.DMA,
            pltpu.SemaphoreType.DMA((E, slices)),
            pltpu.SemaphoreType.DMA((E, slices)),
            pltpu.SemaphoreType.DMA((slices, groups)),
            pltpu.SemaphoreType.DMA((slices, groups)),
        ],
        compiler_params=pltpu.CompilerParams(collective_id=0, has_side_effects=True),
    )(packed)


def slot_rows(target, slot_total, tokens):
    tok_rows = tokens.shape[0]
    slot_table = (target[None, :] == jnp.arange(slot_total, dtype=jnp.int32)[:, None]).astype(
        jnp.int32
    )
    slot_table = jnp.sum(slot_table.reshape(slot_total, tok_rows, 2), axis=2).astype(jnp.bfloat16)
    return jnp.dot(slot_table, tokens, preferred_element_type=jnp.float32).astype(jnp.bfloat16)


def spread(row):
    return jnp.broadcast_to(row, (8, BLK))


def split(value):
    high = value.astype(jnp.bfloat16)
    return high, (value - high.astype(jnp.float32)).astype(jnp.bfloat16)


def tn(a, b):
    return lax.dot_general(a, b, (((0,), (0,)), ((), ())), preferred_element_type=jnp.float32)


def inverse_factor(block_ref, inv_ref, beside):
    lane = lax.broadcasted_iota(jnp.int32, (8, BLK), 1)
    sub = lax.broadcasted_iota(jnp.int32, (8, BLK), 0)
    rest = [block_ref[8 * r : 8 * r + 8, :] for r in range(BLK // 8)]
    count = HALF // 8
    for s in range(BLK // HALF):
        rows, rest = rest[:count], rest[count:]
        dones = []
        for g in range(count):
            first = s * HALF + 8 * g
            inside = (lane >= first) & (lane < first + 8)
            cols = {
                r: [spread_lane(rows[r], first + j) for j in range(8)] for r in range(g, count)
            }
            own = jnp.where(inside, jnp.where(lane == first + sub, 1.0, 0.0), rows[g])
            diag = list(cols[g])
            done = jnp.zeros((8, BLK), jnp.float32)
            for j in range(0, 8, 2):
                u, v = diag[j], diag[j + 1]
                a, b, c = spread(u[j : j + 1]), spread(u[j + 1 : j + 2]), spread(v[j + 1 : j + 2])
                det = a * c - b * b
                recip = 1.0 / det
                root_a = lax.rsqrt(a)
                root_det = lax.rsqrt(det)
                at0, at1 = sub == j, sub == j + 1
                x, y = spread(own[j : j + 1]), spread(own[j + 1 : j + 2])
                lower = a * y - b * x
                upper = c * x - b * y
                done = jnp.where(at0, x * root_a, jnp.where(at1, lower * (root_a * root_det), done))
                sx, sy = upper * recip, lower * recip
                own = jnp.where(at0, sx, jnp.where(at1, sy, own - (u * sx + v * sy)))
                for m in range(j + 2, 8):
                    um, vm = spread(diag[m][j : j + 1]), spread(diag[m][j + 1 : j + 2])
                    p, q = c * um - b * vm, a * vm - b * um
                    w = jnp.where(at0, -p, jnp.where(at1, -q, u * p + v * q))
                    diag[m] = jnp.where(at0 | at1, 0.0, diag[m]) - w * recip
            inv_ref[first : first + 8, :] = jnp.where(lane <= first + sub, done, 0.0)
            dones.append(done)
            parts = [spread(own[j : j + 1, :]) for j in range(8)]
            for r in range(g + 1, count):
                t = [cols[r][j] * parts[j] for j in range(8)]
                t = ((t[0] + t[1]) + (t[2] + t[3])) + ((t[4] + t[5]) + (t[6] + t[7]))
                rows[r] = jnp.where(inside, 0.0, rows[r]) - t
            beside(s * count + g)
        if rest:
            low, top = s * HALF, (s + 1) * HALF
            col = lax.broadcasted_iota(jnp.int32, (HALF, BLK), 1)
            row = lax.broadcasted_iota(jnp.int32, (HALF, BLK), 0) + low
            high, less = split(jnp.where((col <= row) | (col >= top), jnp.concatenate(dones, 0), 0.0))
            taken = tn(jnp.concatenate([high, less, high], 0), jnp.concatenate([high, high, less], 0))
            within = (lane >= low) & (lane < top)
            rest = [
                jnp.where(within, 0.0, value) - taken[top + 8 * r : top + 8 * r + 8, :]
                for r, value in enumerate(rest)
            ]


def spread_lane(value, at):
    return jnp.broadcast_to(value[:, at : at + 1], (8, BLK))


def solve(left, tile):
    high, low = split(tile)
    return jnp.dot(
        left, jnp.concatenate([high, low, high], 0), preferred_element_type=jnp.float32
    )


def upper_part(value, first_row, first_col):
    row = first_row + lax.broadcasted_iota(jnp.int32, value.shape, 0)
    col = first_col + lax.broadcasted_iota(jnp.int32, value.shape, 1)
    return jnp.where(col >= row, value, 0.0).astype(jnp.bfloat16)


def damped(value, first_row, first_col):
    row = first_row + lax.broadcasted_iota(jnp.int32, value.shape, 0)
    col = first_col + lax.broadcasted_iota(jnp.int32, value.shape, 1)
    return value + jnp.where(row == col, damping, 0.0)


def nt(a, b):
    return lax.dot_general(a, b, (((1,), (1,)), ((), ())), preferred_element_type=jnp.float32)


def layer_kernel(
    x_hbm,
    w_hbm,
    out_hbm,
    x_ref,
    w_ref,
    u_ref,
    acc,
    stage,
    wide,
    inverse,
    panel,
    early,
    lefts,
    inv_ref,
    block_ref,
    x_sem,
    w_sem,
    out_sem,
):
    hidden, features = w_hbm.shape
    width = features // NB
    panels = width // BLK
    half = panels // 2
    final = NB - 1
    spare = features
    pieces = hidden // 2

    def at(start, size=BLK):
        return pl.ds(pl.multiple_of(start, BLK), size)

    def band(k):
        return slice(k * width, (k + 1) * width)

    x_copies = [
        pltpu.make_async_copy(x_hbm.at[:, band(k)], x_ref.at[:, band(k)], x_sem.at[k])
        for k in range(NB)
    ]
    w_copy = pltpu.make_async_copy(w_hbm, w_ref, w_sem)
    for copy in x_copies:
        copy.start()
    w_copy.start()

    def clear(r, c):
        u_ref[at(r * BLK), :] = jnp.zeros((BLK, features), jnp.bfloat16)
        return c

    lax.fori_loop(0, features // BLK + 1, clear, 0)
    panel[...] = jnp.zeros_like(panel)
    inverse[...] = jnp.zeros_like(inverse)
    lefts[...] = jnp.zeros_like(lefts)

    def gram(k, own, deep):
        cols = band(k)
        rows = at(k * width + own, TILE)
        value = tn(x_ref[:, rows], x_ref[:, cols])
        if deep:
            value = value - tn(u_ref[:deep, rows], u_ref[:deep, cols])
        wide[k % 2, at(own, TILE), :] = value

    def old(b, k, t):
        cols = at(k * width + t * TILE, TILE)
        value = tn(x_ref[:, band(b)], x_ref[:, cols])
        if b:
            value = value - tn(u_ref[: b * width, band(b)], u_ref[: b * width, cols])
        high, low = split(value)
        own = inverse[b, :width]
        u_ref[band(b), cols] = jnp.dot(
            jnp.concatenate([own, own], 1),
            jnp.concatenate([high, low], 0),
            preferred_element_type=jnp.float32,
        ).astype(jnp.bfloat16)

    def ahead(k, j, kept):
        rows = at(k * width + j * BLK)
        cols = band(k + 1)
        deep = (k + 1) * width
        value = tn(x_ref[:, rows], x_ref[:, cols]) - tn(u_ref[:deep, rows], u_ref[:deep, cols])
        u_ref[at(kept), cols] = solve(lefts[j], value).astype(jnp.bfloat16)

    def invert(k, j, rows):
        row = j * BLK + lax.broadcasted_iota(jnp.int32, (BLK, width), 0)
        col = lax.broadcasted_iota(jnp.int32, (BLK, width), 1)
        value = jnp.where(row == col, 1.0, 0.0) - tn(
            u_ref[band(k), at(k * width + j * BLK)], inverse[k, :width]
        )
        inverse[k, rows] = solve(lefts[j], value).astype(jnp.bfloat16)

    def whiten(j, k, t, m):
        rows = slice(m * pieces, (m + 1) * pieces)
        cols = at(j * width + t * TILE, TILE)
        value = nt(w_ref[rows, band(k)], u_ref[cols, band(k)])
        if k == final:
            w_ref[rows, cols] = (acc[rows, cols] + value).astype(jnp.bfloat16)
        elif j == k:
            acc[rows, cols] = value
        else:
            acc[rows, cols] += value

    def ship(j, t):
        cols = at(j * width + t * TILE, TILE)
        return pltpu.make_async_copy(w_ref.at[:, cols], out_hbm.at[:, cols], out_sem.at[j, t])

    def step(k, i, extra):
        low = k * width
        start = low + i * BLK
        nxt = jnp.minimum(i + 1, panels - 1)
        nxt_at = at(low + nxt * BLK)
        prior = jnp.where(i == 0, panels, i - 1)
        prior_row = jnp.where(i == 0, spare, start - BLK)

        def settle():
            value = solve(lefts[prior], panel[...])
            u_ref[at(prior_row), band(k)] = upper_part(value, start - BLK, low)

        def renew():
            value = wide[k % 2, at(i * BLK), :] - tn(u_ref[band(k), at(start)], u_ref[band(k), band(k)])
            panel[...] = damped(value, start, low)

        def look():
            early[...] = damped(wide[k % 2, at(nxt * BLK), at(nxt * BLK)], 0, 0) - tn(
                u_ref[band(k), nxt_at], u_ref[band(k), nxt_at]
            )

        tasks = [settle, renew, look] + extra
        if k + 2 < NB:
            tasks.append(
                functools.partial(
                    invert,
                    k,
                    jnp.maximum(i - 1, 0),
                    at(jnp.where(i == 0, width, (i - 1) * BLK)),
                )
            )
        slots = BLK // 8

        def beside(g):
            for n, task in enumerate(tasks):
                if n * slots // len(tasks) == g:
                    task()

        inverse_factor(block_ref, inv_ref, beside)
        high, rest = split(inv_ref[...])
        left = jnp.concatenate([high, high, rest], 1)
        lefts[i] = left
        near = upper_part(solve(left, panel[:, at(nxt * BLK)]), start, low + nxt * BLK)
        u_ref[at(start), nxt_at] = near
        block_ref[...] = early[...] - tn(near, near)

    x_copies[0].wait()
    for t in range(0, width, TILE):
        gram(0, t, 0)

    for k in range(NB):
        block_ref[...] = damped(wide[k % 2, 0:BLK, 0:BLK], 0, 0)
        if k < final:
            x_copies[k + 1].wait()
        if k == 1:
            w_copy.wait()

        def first_half(i, c):
            extra = []
            if k < final:
                extra += [functools.partial(old, b, k + 1, i) for b in range(k)]
            if k == 1:
                extra += [functools.partial(whiten, 0, 0, i, m) for m in range(2)]
            if k == final:
                extra += [
                    functools.partial(whiten, j, q, i, m)
                    for q in range(1, final)
                    for j in range(q, -1, -1)
                    if (j, q) != (0, 1)
                    for m in range(2)
                ]
            step(k, i, extra)
            return c

        def second_half(i, c):
            extra = []
            t = i - half
            if k < final:
                for r in range(2):
                    j = 2 * t + r
                    row = jnp.where(j == panels - 1, spare, k * width + j * BLK)
                    extra.append(functools.partial(ahead, k, j, row))
                extra.append(functools.partial(gram, k + 1, t * TILE, k * width))
            if k == 1:
                extra += [functools.partial(whiten, 0, 1, t, m) for m in range(2)]
            if k == final:
                extra += [
                    functools.partial(whiten, j, final, t, m)
                    for j in range(final)
                    for m in range(2)
                ]
            step(k, i, extra)
            if k == final:
                for j in range(final):
                    ship(j, t).start()
            return c

        lax.fori_loop(0, half, first_half, 0)
        lax.fori_loop(half, panels, second_half, 0)
        if k < final:
            ahead(k, panels - 1, (k + 1) * width - BLK)
            for t in range(0, width, TILE):
                wide[(k + 1) % 2, t : t + TILE, :] -= tn(
                    u_ref[band(k), (k + 1) * width + t : (k + 1) * width + t + TILE],
                    u_ref[band(k), band(k + 1)],
                )
            if k + 2 < NB:
                invert(k, panels - 1, at((panels - 1) * BLK))

    last = []
    for t in range(width // TILE):
        here = final * width + t * TILE
        stage[:, t * TILE : (t + 1) * TILE] = nt(
            w_ref[:, here:features], u_ref[here : here + TILE, here:features]
        ).astype(jnp.bfloat16)
        last.append(
            pltpu.make_async_copy(
                stage.at[:, t * TILE : (t + 1) * TILE],
                out_hbm.at[:, here : here + TILE],
                out_sem.at[final, t],
            )
        )
        last[-1].start()
    for j in range(final):
        for t in range(width // TILE):
            ship(j, t).wait()
    for copy in last:
        copy.wait()


def layer(gathered, weights):
    rows, features = gathered.shape
    hidden = weights.shape[0]
    width = features // NB
    panels = width // BLK
    return pl.pallas_call(
        layer_kernel,
        out_shape=jax.ShapeDtypeStruct((hidden, features), jnp.bfloat16),
        in_specs=[pl.BlockSpec(memory_space=pltpu.HBM)] * 2,
        out_specs=pl.BlockSpec(memory_space=pltpu.HBM),
        scratch_shapes=[
            pltpu.VMEM((rows, features), jnp.bfloat16),
            pltpu.VMEM((hidden, features), jnp.bfloat16),
            pltpu.VMEM((features + BLK, features), jnp.bfloat16),
            pltpu.VMEM((hidden, features - width), jnp.float32),
            pltpu.VMEM((hidden, width), jnp.bfloat16),
            pltpu.VMEM((2, width, width), jnp.float32),
            pltpu.VMEM((NB - 2, width + BLK, width), jnp.bfloat16),
            pltpu.VMEM((BLK, width), jnp.float32),
            pltpu.VMEM((BLK, BLK), jnp.float32),
            pltpu.VMEM((panels + 1, BLK, 3 * BLK), jnp.bfloat16),
            pltpu.VMEM((BLK, BLK), jnp.float32),
            pltpu.VMEM((BLK, BLK), jnp.float32),
            pltpu.SemaphoreType.DMA((NB,)),
            pltpu.SemaphoreType.DMA,
            pltpu.SemaphoreType.DMA((NB, width // TILE)),
        ],
        compiler_params=pltpu.CompilerParams(vmem_limit_bytes=63 << 20),
    )(gathered, weights)


def local(tokens, routes, weights):
    tok_devices = lax.axis_size("tok")
    tok_rows = tokens.shape[0]
    features = tokens.shape[1]
    most_rows = tok_rows * 5 // 16
    picked = routes.reshape(-1)
    onehot = (picked[:, None] == jnp.arange(E, dtype=jnp.int32)[None, :]).astype(jnp.bfloat16)
    place = jnp.arange(2 * tok_rows, dtype=jnp.int32)
    earlier = (place[:, None] > place[None, :]).astype(jnp.bfloat16)
    before = jnp.dot(earlier, onehot, preferred_element_type=jnp.float32)
    ranked = jnp.sum(before * onehot.astype(jnp.float32), axis=1).astype(jnp.int32)
    packed = slot_rows(picked * most_rows + ranked, E * most_rows, tokens)
    gathered = exchange(packed.reshape(E, most_rows, features), tok_devices)
    return layer(gathered.reshape(tok_devices * most_rows, features), weights)


def solution(mesh):
    return jax.shard_map(
        local,
        mesh=mesh,
        in_specs=(
            P(("groups", "tok"), None),
            P(("groups", "tok"), None),
            P(("groups", "tok"), None),
        ),
        out_specs=P(("groups", "tok"), None),
        check_vma=False,
    )
```

```python
import functools

import jax
import jax.numpy as jnp
from jax import lax
from jax.experimental import pallas as pl
from jax.experimental.pallas import tpu as pltpu
from jax.sharding import PartitionSpec as P

E = 8
NB = 4
BLK = 128
TILE = 256
HALF = 64

damping = 256.0


def slot_rows(target, slot_total, tokens):
    tok_rows = tokens.shape[0]
    slot_table = (target[None, :] == jnp.arange(slot_total, dtype=jnp.int32)[:, None]).astype(
        jnp.int32
    )
    slot_table = jnp.sum(slot_table.reshape(slot_total, tok_rows, 2), axis=2).astype(jnp.bfloat16)
    return jnp.dot(slot_table, tokens, preferred_element_type=jnp.float32).astype(jnp.bfloat16)


def spread(row):
    return jnp.broadcast_to(row, (8, BLK))


def split(value):
    high = value.astype(jnp.bfloat16)
    return high, (value - high.astype(jnp.float32)).astype(jnp.bfloat16)


def tn(a, b):
    return lax.dot_general(a, b, (((0,), (0,)), ((), ())), preferred_element_type=jnp.float32)


def inverse_factor(block_ref, inv_ref, beside):
    lane = lax.broadcasted_iota(jnp.int32, (8, BLK), 1)
    sub = lax.broadcasted_iota(jnp.int32, (8, BLK), 0)
    rest = [block_ref[8 * r : 8 * r + 8, :] for r in range(BLK // 8)]
    count = HALF // 8
    for s in range(BLK // HALF):
        rows, rest = rest[:count], rest[count:]
        dones = []
        following = None
        for g in range(count):
            first = s * HALF + 8 * g
            inside = (lane >= first) & (lane < first + 8)
            cols = {
                r: [spread_lane(rows[r], first + j) for j in range(8)]
                for r in range(g if following is None else g + 1, count)
            }
            own = jnp.where(inside, jnp.where(lane == first + sub, 1.0, 0.0), rows[g])
            diag = list(cols[g]) if following is None else following
            following = None
            if g + 1 < count:
                under = list(cols[g + 1])
                following = [spread_lane(rows[g + 1], first + 8 + j) for j in range(8)]
            done = jnp.zeros((8, BLK), jnp.float32)
            for j in range(0, 8, 2):
                u, v = diag[j], diag[j + 1]
                a, b, c = spread(u[j : j + 1]), spread(u[j + 1 : j + 2]), spread(v[j + 1 : j + 2])
                det = a * c - b * b
                recip = 1.0 / det
                root_a = lax.rsqrt(a)
                root_det = lax.rsqrt(det)
                at0, at1 = sub == j, sub == j + 1
                x, y = spread(own[j : j + 1]), spread(own[j + 1 : j + 2])
                lower = a * y - b * x
                upper = c * x - b * y
                done = jnp.where(at0, x * root_a, jnp.where(at1, lower * (root_a * root_det), done))
                sx, sy = upper * recip, lower * recip
                own = jnp.where(at0, sx, jnp.where(at1, sy, own - (u * sx + v * sy)))
                if following is not None:
                    nu, nv = under[j], under[j + 1]
                    su, sv = (c * nu - b * nv) * recip, (a * nv - b * nu) * recip
                    following = [
                        value - (su * spread(nu[n : n + 1]) + sv * spread(nv[n : n + 1]))
                        for n, value in enumerate(following)
                    ]
                for m in range(j + 2, 8):
                    um, vm = spread(diag[m][j : j + 1]), spread(diag[m][j + 1 : j + 2])
                    if following is not None:
                        under[m] = under[m] - (su * um + sv * vm)
                    p, q = c * um - b * vm, a * vm - b * um
                    w = jnp.where(at0, -p, jnp.where(at1, -q, u * p + v * q))
                    diag[m] = jnp.where(at0 | at1, 0.0, diag[m]) - w * recip
            inv_ref[first : first + 8, :] = jnp.where(lane <= first + sub, done, 0.0)
            dones.append(done)
            parts = [spread(own[j : j + 1, :]) for j in range(8)]
            for r in range(g + 1, count):
                t = [cols[r][j] * parts[j] for j in range(8)]
                t = ((t[0] + t[1]) + (t[2] + t[3])) + ((t[4] + t[5]) + (t[6] + t[7]))
                rows[r] = jnp.where(inside, 0.0, rows[r]) - t
            beside(s * count + g)
        if rest:
            low, top = s * HALF, (s + 1) * HALF
            col = lax.broadcasted_iota(jnp.int32, (HALF, BLK), 1)
            row = lax.broadcasted_iota(jnp.int32, (HALF, BLK), 0) + low
            high, less = split(jnp.where((col <= row) | (col >= top), jnp.concatenate(dones, 0), 0.0))
            taken = tn(jnp.concatenate([high, less, high], 0), jnp.concatenate([high, high, less], 0))
            within = (lane >= low) & (lane < top)
            rest = [
                jnp.where(within, 0.0, value) - taken[top + 8 * r : top + 8 * r + 8, :]
                for r, value in enumerate(rest)
            ]


def spread_lane(value, at):
    return jnp.broadcast_to(value[:, at : at + 1], (8, BLK))


def solve(left, tile):
    high, low = split(tile)
    return jnp.dot(
        left, jnp.concatenate([high, low, high], 0), preferred_element_type=jnp.float32
    )


def upper_part(value, first_row, first_col):
    row = first_row + lax.broadcasted_iota(jnp.int32, value.shape, 0)
    col = first_col + lax.broadcasted_iota(jnp.int32, value.shape, 1)
    return jnp.where(col >= row, value, 0.0).astype(jnp.bfloat16)


def damped(value, first_row, first_col):
    row = first_row + lax.broadcasted_iota(jnp.int32, value.shape, 0)
    col = first_col + lax.broadcasted_iota(jnp.int32, value.shape, 1)
    return value + jnp.where(row == col, damping, 0.0)


def nt(a, b):
    return lax.dot_general(a, b, (((1,), (1,)), ((), ())), preferred_element_type=jnp.float32)


def layer_kernel(
    slices,
    per,
    packed,
    w_hbm,
    out_hbm,
    landing,
    x_ref,
    w_ref,
    u_ref,
    acc,
    wide,
    inverse,
    panel,
    late,
    early,
    lefts,
    inv_ref,
    block_ref,
    x_sem,
    w_sem,
    out_sem,
    own_sem,
    send,
    recv,
    pass_send,
    pass_recv,
):
    most = packed.shape[1]
    count = E * slices
    me = lax.axis_index("tok")
    mine = lax.rem(me, slices)
    expert = me // slices
    sizes = [max(0, min(per, most - s * per)) for s in range(slices)]
    hidden, features = w_hbm.shape
    width = features // NB
    panels = width // BLK
    half = panels // 2
    final = NB - 1
    spare = features
    pieces = hidden // 2

    def at(start, size=BLK):
        return pl.ds(pl.multiple_of(start, BLK), size)

    def band(k):
        return slice(k * width, (k + 1) * width)

    def landed(s, size, block):
        return pl.ds(pl.multiple_of(count * per * s + block * size, 8), size)

    def routed(c, eo, s, size, recv_slot):
        to = lax.rem(expert + eo, E)
        return pltpu.make_async_remote_copy(
            src_ref=packed.at[to, pl.ds(s * per, size), band(c)],
            dst_ref=landing.at[landed(s, size, eo * slices + mine), band(c)],
            send_sem=send.at[c, eo, s],
            recv_sem=recv.at[c, eo, recv_slot],
            device_id={"tok": to * slices + s},
            device_id_type=pl.DeviceIdType.MESH,
        )

    def kept(c, s, size):
        return pltpu.make_async_copy(
            packed.at[expert, pl.ds(s * per, size), band(c)],
            landing.at[landed(s, size, mine), band(c)],
            own_sem.at[c],
        )

    def shared(c, p, s, size):
        part = (pl.ds(count * per * s, count * size), band(c))
        return pltpu.make_async_remote_copy(
            src_ref=landing.at[part],
            dst_ref=landing.at[part],
            send_sem=pass_send.at[c, p],
            recv_sem=pass_recv.at[c, s],
            device_id={"tok": expert * slices + p},
            device_id_type=pl.DeviceIdType.MESH,
        )

    barrier = pltpu.get_barrier_semaphore()
    for d in range(1, count):
        pl.semaphore_signal(
            barrier,
            inc=1,
            device_id={"tok": lax.rem(me + d, count)},
            device_id_type=pl.DeviceIdType.MESH,
        )
    pl.semaphore_wait(barrier, count - 1)

    def each_slot(same, other):
        for s, size in enumerate(sizes):
            if size:
                pl.when(mine == s)(functools.partial(same, s, size))
                pl.when(mine != s)(functools.partial(other, s, size))

    def begin(c):
        for eo in range(1, E):
            for s, size in enumerate(sizes):
                if size:
                    routed(c, eo, s, size, mine).start()
        each_slot(
            lambda s, size: kept(c, s, size).start(),
            lambda s, size: routed(c, 0, s, size, mine).start(),
        )

    def receive(c):
        def same(s, size):
            for eo in range(E):
                for other in range(slices):
                    if eo or other != s:
                        routed(c, eo, s, size, other).wait_recv()
            kept(c, s, size).wait()
            for p in range(slices):
                if p != s:
                    shared(c, p, s, size).start()

        each_slot(same, lambda s, size: None)

    def complete(c):
        each_slot(lambda s, size: None, lambda s, size: shared(c, s, s, size).wait_recv())
        x_copies[c].start()

    def left(c):
        for eo in range(1, E):
            for s, size in enumerate(sizes):
                if size:
                    routed(c, eo, s, size, mine).wait_send()
        each_slot(
            lambda s, size: None, lambda s, size: routed(c, 0, s, size, mine).wait_send()
        )

    def passed(c):
        def same(s, size):
            for p in range(slices):
                if p != s:
                    shared(c, p, s, size).wait_send()

        each_slot(same, lambda s, size: None)

    begin(0)

    x_copies = [
        pltpu.make_async_copy(landing.at[:, band(k)], x_ref.at[:, band(k)], x_sem.at[k])
        for k in range(NB)
    ]
    w_copy = pltpu.make_async_copy(w_hbm, w_ref, w_sem)

    def clear(r, c):
        u_ref[at(r * BLK), :] = jnp.zeros((BLK, features), jnp.bfloat16)
        return c

    lax.fori_loop(0, features // BLK + 1, clear, 0)
    panel[...] = jnp.zeros_like(panel)
    inverse[...] = jnp.zeros_like(inverse)
    lefts[...] = jnp.zeros_like(lefts)

    def gram(k, own, deep):
        cols = band(k)
        rows = at(k * width + own, TILE)
        value = tn(x_ref[:, rows], x_ref[:, cols])
        if deep:
            value = value - tn(u_ref[:deep, rows], u_ref[:deep, cols])
        wide[k % 2, at(own, TILE), :] = value

    def old(b, k, t):
        cols = at(k * width + t * TILE, TILE)
        value = tn(x_ref[:, band(b)], x_ref[:, cols])
        if b:
            value = value - tn(u_ref[: b * width, band(b)], u_ref[: b * width, cols])
        high, low = split(value)
        own = inverse[b, :width]
        u_ref[band(b), cols] = jnp.dot(
            jnp.concatenate([own, own], 1),
            jnp.concatenate([high, low], 0),
            preferred_element_type=jnp.float32,
        ).astype(jnp.bfloat16)

    def right_side(k, j):
        rows = at(k * width + j * BLK)
        cols = band(k + 1)
        deep = (k + 1) * width
        return tn(x_ref[:, rows], x_ref[:, cols]) - tn(u_ref[:deep, rows], u_ref[:deep, cols])

    def ahead(k, j):
        value = solve(lefts[j], right_side(k, j))
        u_ref[at(k * width + j * BLK), band(k + 1)] = value.astype(jnp.bfloat16)

    def ahead_or_hold(k, j):
        late[...] = right_side(k, j)
        row = jnp.where(j == panels - 1, spare, k * width + j * BLK)
        u_ref[at(row), band(k + 1)] = solve(lefts[j], late[...]).astype(jnp.bfloat16)

    def invert(k, j, rows):
        row = j * BLK + lax.broadcasted_iota(jnp.int32, (BLK, width), 0)
        col = lax.broadcasted_iota(jnp.int32, (BLK, width), 1)
        value = jnp.where(row == col, 1.0, 0.0) - tn(
            u_ref[band(k), at(k * width + j * BLK)], inverse[k, :width]
        )
        inverse[k, rows] = solve(lefts[j], value).astype(jnp.bfloat16)

    def whiten(j, k, t, m):
        rows = slice(m * pieces, (m + 1) * pieces)
        cols = at(j * width + t * TILE, TILE)
        value = nt(w_ref[rows, band(k)], u_ref[cols, band(k)])
        if k == final:
            w_ref[rows, cols] = (acc[rows, cols] + value).astype(jnp.bfloat16)
        elif j == k:
            acc[rows, cols] = value
        else:
            acc[rows, cols] += value

    def ship(j, t):
        cols = at(j * width + t * TILE, TILE)
        return pltpu.make_async_copy(w_ref.at[:, cols], out_hbm.at[:, cols], out_sem.at[j, t])

    def step(k, i, extra):
        low = k * width
        start = low + i * BLK
        nxt = jnp.minimum(i + 1, panels - 1)
        nxt_at = at(low + nxt * BLK)
        prior = jnp.where(i == 0, panels, i - 1)
        prior_row = jnp.where(i == 0, spare, start - BLK)

        def settle():
            value = solve(lefts[prior], panel[...])
            u_ref[at(prior_row), band(k)] = upper_part(value, start - BLK, low)

        def renew():
            value = wide[k % 2, at(i * BLK), :] - tn(u_ref[band(k), at(start)], u_ref[band(k), band(k)])
            panel[...] = damped(value, start, low)

        def look():
            early[...] = damped(wide[k % 2, at(nxt * BLK), at(nxt * BLK)], 0, 0) - tn(
                u_ref[band(k), nxt_at], u_ref[band(k), nxt_at]
            )

        tasks = [settle, renew, look] + extra
        if k + 2 < NB:
            tasks.append(
                functools.partial(
                    invert,
                    k,
                    jnp.maximum(i - 1, 0),
                    at(jnp.where(i == 0, width, (i - 1) * BLK)),
                )
            )
        slots = BLK // 8

        def beside(g):
            for n, task in enumerate(tasks):
                if n * slots // len(tasks) == g:
                    task()

        inverse_factor(block_ref, inv_ref, beside)
        high, rest = split(inv_ref[...])
        left = jnp.concatenate([high, high, rest], 1)
        lefts[i] = left
        near = upper_part(solve(left, panel[:, at(nxt * BLK)]), start, low + nxt * BLK)
        u_ref[at(start), nxt_at] = near
        block_ref[...] = early[...] - tn(near, near)

    left(0)
    begin(1)
    receive(0)
    complete(0)
    w_copy.start()
    x_copies[0].wait()
    for t in range(0, width, TILE):
        gram(0, t, 0)

    for k in range(NB):
        block_ref[...] = damped(wide[k % 2, 0:BLK, 0:BLK], 0, 0)
        if 0 < k < final:
            x_copies[k + 1].wait()
        if k == 1:
            w_copy.wait()

        def first_half(i, c):
            extra = []
            if k < 2:
                pl.when(i == half - 1)(functools.partial(receive, 2 * k + 1))
                if k == 0:
                    pl.when(i == half - 1)(functools.partial(begin, 2))
            if k < final:
                extra += [functools.partial(old, b, k + 1, i) for b in range(k)]
            if k == 1:
                extra += [functools.partial(whiten, 0, 0, i, m) for m in range(2)]
            if k == final:
                extra += [
                    functools.partial(whiten, j, q, i, m)
                    for q in range(1, final)
                    for j in range(q, -1, -1)
                    if (j, q) != (0, 1)
                    for m in range(2)
                ]
            step(k, i, extra)
            return c

        def second_half(i, c):
            extra = []
            t = i - half
            if k == 0:
                pl.when(i == half + 1)(functools.partial(receive, 2))
                pl.when(i == half + 1)(functools.partial(begin, 3))
                pl.when(i == half + 2)(functools.partial(complete, 2))
            if k < final:
                extra.append(functools.partial(ahead, k, 2 * t))
                extra.append(functools.partial(ahead_or_hold, k, 2 * t + 1))
                extra.append(functools.partial(gram, k + 1, t * TILE, k * width))
            if k == 1:
                extra += [functools.partial(whiten, 0, 1, t, m) for m in range(2)]
            if k == final:
                extra += [
                    functools.partial(whiten, j, final, t, m)
                    for j in range(final)
                    for m in range(2)
                ]
            step(k, i, extra)
            if k == final:
                for j in range(final):
                    ship(j, t).start()
            return c

        lax.fori_loop(0, half, first_half, 0)
        if k < 2:
            complete(2 * k + 1)
        if k == 0:
            x_copies[1].wait()
        lax.fori_loop(half, panels, second_half, 0)
        if k < final:
            u_ref[(k + 1) * width - BLK : (k + 1) * width, band(k + 1)] = solve(
                lefts[panels - 1], late[...]
            ).astype(jnp.bfloat16)
            for t in range(0, width, TILE):
                wide[(k + 1) % 2, t : t + TILE, :] -= tn(
                    u_ref[band(k), (k + 1) * width + t : (k + 1) * width + t + TILE],
                    u_ref[band(k), band(k + 1)],
                )
            if k + 2 < NB:
                invert(k, panels - 1, at((panels - 1) * BLK))

    last = []
    for t in range(width // TILE):
        here = final * width + t * TILE
        u_ref[:hidden, t * TILE : (t + 1) * TILE] = nt(
            w_ref[:, here:features], u_ref[here : here + TILE, here:features]
        ).astype(jnp.bfloat16)
        last.append(
            pltpu.make_async_copy(
                u_ref.at[:hidden, t * TILE : (t + 1) * TILE],
                out_hbm.at[:, here : here + TILE],
                out_sem.at[final, t],
            )
        )
        last[-1].start()
    for j in range(final):
        for t in range(width // TILE):
            ship(j, t).wait()
    for copy in last:
        copy.wait()
    for c in range(NB):
        if c:
            left(c)
        passed(c)


def layer(packed, weights, slices):
    _, most, features = packed.shape
    per = -(-most // 8 // slices) * 8
    rows = E * slices * most
    hidden = weights.shape[0]
    width = features // NB
    panels = width // BLK
    return pl.pallas_call(
        functools.partial(layer_kernel, slices, per),
        out_shape=(
            jax.ShapeDtypeStruct((hidden, features), jnp.bfloat16),
            jax.ShapeDtypeStruct((rows, features), jnp.bfloat16),
        ),
        in_specs=[pl.BlockSpec(memory_space=pltpu.HBM)] * 2,
        out_specs=(pl.BlockSpec(memory_space=pltpu.HBM),) * 2,
        scratch_shapes=[
            pltpu.VMEM((rows, features), jnp.bfloat16),
            pltpu.VMEM((hidden, features), jnp.bfloat16),
            pltpu.VMEM((features + BLK, features), jnp.bfloat16),
            pltpu.VMEM((hidden, features - width), jnp.float32),
            pltpu.VMEM((2, width, width), jnp.float32),
            pltpu.VMEM((NB - 2, width + BLK, width), jnp.bfloat16),
            pltpu.VMEM((BLK, width), jnp.float32),
            pltpu.VMEM((BLK, width), jnp.float32),
            pltpu.VMEM((BLK, BLK), jnp.float32),
            pltpu.VMEM((panels + 1, BLK, 3 * BLK), jnp.bfloat16),
            pltpu.VMEM((BLK, BLK), jnp.float32),
            pltpu.VMEM((BLK, BLK), jnp.float32),
            pltpu.SemaphoreType.DMA((NB,)),
            pltpu.SemaphoreType.DMA,
            pltpu.SemaphoreType.DMA((NB, width // TILE)),
            pltpu.SemaphoreType.DMA((NB,)),
            pltpu.SemaphoreType.DMA((NB, E, slices)),
            pltpu.SemaphoreType.DMA((NB, E, slices)),
            pltpu.SemaphoreType.DMA((NB, slices)),
            pltpu.SemaphoreType.DMA((NB, slices)),
        ],
        compiler_params=pltpu.CompilerParams(
            collective_id=0, has_side_effects=True, vmem_limit_bytes=63 << 20
        ),
    )(packed, weights)[0]


def local(tokens, routes, weights):
    tok_devices = lax.axis_size("tok")
    tok_rows = tokens.shape[0]
    features = tokens.shape[1]
    most_rows = tok_rows * 5 // 16
    picked = routes.reshape(-1)
    onehot = (picked[:, None] == jnp.arange(E, dtype=jnp.int32)[None, :]).astype(jnp.bfloat16)
    place = jnp.arange(2 * tok_rows, dtype=jnp.int32)
    earlier = (place[:, None] > place[None, :]).astype(jnp.bfloat16)
    before = jnp.dot(earlier, onehot, preferred_element_type=jnp.float32)
    ranked = jnp.sum(before * onehot.astype(jnp.float32), axis=1).astype(jnp.int32)
    packed = slot_rows(picked * most_rows + ranked, E * most_rows, tokens)
    return layer(packed.reshape(E, most_rows, features), weights, tok_devices // E)


def solution(mesh):
    return jax.shard_map(
        local,
        mesh=mesh,
        in_specs=(
            P(("groups", "tok"), None),
            P(("groups", "tok"), None),
            P(("groups", "tok"), None),
        ),
        out_specs=P(("groups", "tok"), None),
        check_vma=False,
    )
```
